512 devices in a mesh: vocab: 64 (over x, z), batch: 8 (over y, core).
Axes of the slice: x: 4, y: 4, z: 16, core: 2. Of those that a mesh axis runs over, the one named last changes fastest.
Arguments:
- hidden: bfloat16 [1024, 4096], P('batch', 'vocab'), may hold values from -6 to 6
- head_weight: bfloat16 [4096, 65536], P('batch', 'vocab'), may hold values from -0.09375 to 0.09375
- passages: bfloat16 [2048, 65536], P('batch', 'vocab'), may hold values from -6 to 6
- pair_query: int32 [3072], P('batch'), may hold values from 0 to 63
- pair_passage: int32 [3072], P('batch'), may hold values from 0 to 255
- pair_count: int32 [8], P('batch'), may hold values from 128 to 384, as said below
- teacher: float32 [3072], P('batch'), may hold values from -24 to 24
Outputs:
- pooled: bfloat16 [64, 65536], P('batch', 'vocab')
- grad_hidden: bfloat16 [1024, 4096], P('batch', 'vocab')
- loss_value: float32 [], replicated
The draws below stay inside these ranges and needn't reach their ends.
Inputs may be any that keep to these rules, and one draw needn't show every extreme that they name: `pair_count`: slots of a group at or past its count are padding; some group has all 384 slots live.
All inputs are finite; a program needn't handle non-finite values.
Results may differ from the reference program's by a relative error of at most 0.012.
Values may be sent and summed in bfloat16 or wider, within the bound.
No kernel may reach another device: no remote copies, remote signals or barrier semaphores. Data moves between devices by JAX's collectives and lax.ppermute only.
A program may use at most 64 MiB of HBM per device.

```python
import math
import jax
import jax.numpy as jnp
from jax import lax

D = 4096
VOCAB = 65536
QLEN = 16
PG = 256
SLOTS = 384
TOKENS = 1024
QUERIES = 64
PASSAGES = 2048
N_BATCH = 8


def draw_pair_count(key, part):
    first_key = jax.random.fold_in(key, 11)
    second_key = jax.random.fold_in(key, 23)
    counts = jax.random.randint(first_key, (N_BATCH,), SLOTS // 3, SLOTS + 1)
    chosen = jax.random.randint(second_key, (), 0, N_BATCH)
    return jnp.where(jnp.arange(N_BATCH) == chosen, SLOTS, counts).astype(jnp.int32)


def touch_ends(array, stream_key, least, high):
    longest = array.shape.index(max(array.shape))
    spots = []
    for shift in (0, 1):
        where = [jax.random.randint(jax.random.fold_in(stream_key, axis), (), 0, length) for axis, length in enumerate(array.shape)]
        where[longest] = (where[longest] + shift) % array.shape[longest]
        spots.append(tuple(where))
    return array.at[spots[0]].set(least).at[spots[1]].set(high)


def steps_of(stream_key, shape, cuts, smallest, high):
    factor_of, own = 1.0, jax.random.fold_in(stream_key, 6)
    for dim, blocks in cuts:
        heights = jnp.exp(jax.random.uniform(jax.random.fold_in(own, dim), (blocks,), jnp.float32, smallest / len(cuts), high / len(cuts)))
        factor_of = factor_of * jnp.repeat(heights, shape[dim] // blocks).reshape([-1 if axis == dim else 1 for axis in range(len(shape))])
    return factor_of


def bell_draw(own_key, extent, scale, limit, shards=(), kind=jnp.bfloat16):
    drawn = scale * jax.random.normal(own_key, extent, jnp.float32)
    if shards:
        drawn = drawn * steps_of(own_key, extent, shards, -0.22, 0.18)
    return jnp.clip(drawn, -limit, limit).astype(kind)


def setup_inputs(seed: int = 0) -> dict:
    key_list = jax.random.split(jax.random.key(seed), 8)
    return {
        "hidden": bell_draw(key_list[0], (TOKENS, D), 1.0, 6.0, ((0, 8), (1, 64))),
        "head_weight": bell_draw(key_list[1], (D, VOCAB), D ** -0.5, 0.09375, ((0, 8), (1, 64))),
        "passages": bell_draw(key_list[2], (PASSAGES, VOCAB), 1.0, 6.0, ((0, 8), (1, 64))),
        "pair_query": touch_ends(jax.random.randint(key_list[3], (N_BATCH * SLOTS,), 0, QUERIES), jax.random.fold_in(key_list[3], 1), 0, QUERIES - 1).astype(jnp.int32),
        "pair_passage": touch_ends(jax.random.randint(key_list[4], (N_BATCH * SLOTS,), 0, PG), jax.random.fold_in(key_list[4], 1), 0, PG - 1).astype(jnp.int32),
        "pair_count": draw_pair_count(jax.random.fold_in(key_list[7], 71), 0),
        "teacher": bell_draw(key_list[6], (N_BATCH * SLOTS,), 4.0, 24.0, ((0, 8),), jnp.float32),
    }


def saturate(logits):
    positive = jnp.maximum(logits, 0.0)
    return (jnp.log1p(positive), jnp.where(logits > 0, 1.0 / (1.0 + positive), 0.0))

def reference(hidden, head_weight, passages, pair_query, pair_passage, pair_count, teacher):
    block_size = math.gcd(VOCAB, 4096)
    block_count = VOCAB // block_size
    head_blocks = head_weight.reshape(D, block_count, block_size).transpose(1, 0, 2)

    def forward_block(weights):
        logits = jnp.dot(hidden, weights, preferred_element_type=jnp.float32)
        saturated, unused = saturate(logits)
        return saturated.reshape(QUERIES, QLEN, block_size).sum(1).astype(jnp.bfloat16)
    pooled_blocks = lax.map(forward_block, head_blocks)
    pooled = pooled_blocks.transpose(1, 0, 2).reshape(QUERIES, VOCAB)
    score_table = jnp.dot(pooled, passages.T, preferred_element_type=jnp.float32)
    inv_root = 1.0 / math.sqrt(VOCAB)
    slot_ids = jnp.arange(N_BATCH * SLOTS, dtype=jnp.int32)
    group_index = slot_ids // SLOTS
    slot_index = slot_ids % SLOTS
    global_passage = (group_index * PG + pair_passage).astype(jnp.int32)
    scores = score_table[pair_query, global_passage] * inv_root
    is_live = slot_index < pair_count[group_index]
    residual = jnp.where(is_live, scores - teacher, 0.0)
    loss_value = jnp.sum(residual * residual) / (SLOTS * N_BATCH)
    pair_grad = 2.0 * residual * inv_root
    pair_table = jnp.zeros((QUERIES, PASSAGES), jnp.float32).at[pair_query, global_passage].add(pair_grad)
    query_grad = jnp.dot(pair_table, passages.astype(jnp.float32), precision=lax.Precision.HIGHEST)
    query_blocks = query_grad.reshape(QUERIES, block_count, block_size).transpose(1, 0, 2)

    def backward_block(carry, items):
        weights, query_block = items
        logits = jnp.dot(hidden, weights, preferred_element_type=jnp.float32)
        unused, slope_term = saturate(logits)
        logit_grad = (jnp.repeat(query_block, QLEN, axis=0) * slope_term).astype(jnp.bfloat16)
        return (carry + jnp.dot(logit_grad, weights.T, preferred_element_type=jnp.float32), None)
    grad_total, unused = lax.scan(backward_block, jnp.zeros((TOKENS, D), jnp.float32), (head_blocks, query_blocks))
    return (pooled, grad_total.astype(jnp.bfloat16), loss_value)
```

```python
import math

import jax
import jax.numpy as jnp
from jax import lax
from jax.sharding import Mesh
from jax.sharding import PartitionSpec as P

VOCAB = 65536
QLEN = 16
F32 = jnp.float32
BF16 = jnp.bfloat16


def ring(n, step):
    return [(i, (i + step) % n) for i in range(n)]


def spread(value, axes, n):
    return lax.all_to_all(jnp.broadcast_to(value[None], (n,) + value.shape), axes, 0, 0, tiled=True)


def dot(a, b, ca, cb):
    return lax.dot_general(a, b, (((ca,), (cb,)), ((), ())), preferred_element_type=F32)


def local(hidden, head, passages, pair_query, pair_passage, pair_count, teacher):
    nx, nz = lax.axis_size("x"), lax.axis_size("z")
    ny, nc = lax.axis_size("y"), lax.axis_size("c")
    y, c = lax.axis_index("y"), lax.axis_index("c")
    tok, feat = hidden.shape
    rows, cols = head.shape
    half = rows // 2
    batch = ny * nc
    queries = tok // QLEN

    plus, minus = ring(ny, 1), ring(ny, ny - 1)
    top, low = head[:half], head[half:]
    prev_top = lax.ppermute(top, "y", plus)
    next_low = lax.ppermute(low, "y", minus)
    prev_low = lax.ppermute(low, "y", plus)
    next_top = lax.ppermute(top, "y", minus)
    far_top = lax.ppermute(prev_top, "y", plus)
    far_low = lax.ppermute(next_low, "y", minus)

    part = spread(hidden.T, "z", nz).reshape(nz * feat, tok)
    features = spread(part, "x", nx).reshape(nx * nz * feat, tok)

    mine = [
        (0, 0, head, rows),
        (ny - 1, 0, prev_top, half),
        (ny - 1, half, prev_low, half),
        (1, 0, next_top, half),
        (1, half, next_low, half),
        (2, 0, far_top, half),
        (2, half, far_low, half),
    ]
    swap = ring(nc, 1)
    blocks = []
    for step, start, block, size in mine:
        blocks.append((step, 0, start, block, size))
        blocks.append((step, 1, start, lax.ppermute(block, "c", swap), size))

    logits = None
    for step, other, start, block, size in blocks:
        owner = lax.rem(y + step, ny) * nc + lax.rem(c + other, nc)
        lhs = lax.dynamic_slice_in_dim(features, owner * rows + start, size, 0)
        term = dot(lhs, block, 0, 0)
        logits = term if logits is None else logits + term

    positive = jnp.maximum(logits, 0.0)
    pooled = jnp.log1p(positive).reshape(queries, QLEN, cols).sum(1).astype(BF16)
    every_query = spread(pooled, ("y", "c"), batch).reshape(batch * queries, cols)

    inv_root = 1.0 / math.sqrt(VOCAB)
    slots = pair_query.shape[0]
    n_query, n_passage = every_query.shape[0], passages.shape[0]
    table = dot(passages, every_query, 1, 1)
    query_hot = (pair_query[None, :] == jnp.arange(n_query, dtype=jnp.int32)[:, None]).astype(F32)
    passage_hot = (
        pair_passage[None, :] == jnp.arange(n_passage, dtype=jnp.int32)[:, None]
    ).astype(F32)
    spread_table = jnp.dot(table, query_hot, precision=lax.Precision.HIGHEST)
    partial_value = (spread_table * passage_hot).sum(0)
    packed = jnp.pad(partial_value, (0, -slots % 512)).reshape(-1, 128)
    packed = spread(packed, "x", nx).sum(0)
    packed = spread(packed, "z", nz).sum(0)
    scores = packed.reshape(-1)[:slots] * inv_root

    is_live = jnp.arange(slots, dtype=jnp.int32) < pair_count[0]
    residual = jnp.where(is_live, scores - teacher, 0.0)
    error = jnp.sum(residual * residual)
    pair_grad = 2.0 * residual * inv_root
    pair_table = lax.dot_general(
        query_hot,
        passage_hot * pair_grad[None, :],
        (((1,), (1,)), ((), ())),
        precision=lax.Precision.HIGHEST,
    )
    table_high = pair_table.astype(BF16)
    table_low = (pair_table - table_high.astype(F32)).astype(BF16)
    query_terms = dot(table_high, passages, 1, 0) + dot(table_low, passages, 1, 0)
    terms = jnp.concatenate(
        [
            query_terms.reshape(batch, queries, cols),
            jnp.broadcast_to(error, (batch, queries, 128)),
        ],
        axis=2,
    )
    terms = lax.all_to_all(terms, ("y", "c"), 0, 0, tiled=True).sum(0)
    query_grad = terms[:, :cols]
    loss_value = terms[0, cols] / (slots * batch)

    slope = jnp.where(logits > 0, 1.0 / (1.0 + positive), 0.0)
    logit_grad = (jnp.repeat(query_grad, QLEN, axis=0) * slope).astype(BF16)

    order = []
    for step in range(ny):
        pair = []
        for other in range(nc):
            for want, has, start, block, size in blocks:
                if want == step and has == other:
                    pair.append(dot(block, logit_grad, 1, 1).astype(BF16))
        first = jnp.concatenate(pair[: len(pair) // 2], axis=0)
        second = jnp.concatenate(pair[len(pair) // 2 :], axis=0)
        order.append(
            jnp.concatenate([jnp.where(c == 0, first, second), jnp.where(c == 0, second, first)])
        )
    relative = jnp.stack(order + order)
    hidden_terms = lax.dynamic_slice_in_dim(relative, lax.rem(ny - y, ny), ny, 0)
    hidden_terms = hidden_terms.reshape(nx, nz * feat, tok)
    over_x = lax.all_to_all(hidden_terms, "x", 0, 0, tiled=True)
    over_x = over_x.astype(F32).sum(0).astype(BF16).reshape(nz, feat, tok)
    over_z = lax.all_to_all(over_x, "z", 0, 0, tiled=True)
    grad_hidden = over_z.astype(F32).sum(0).astype(BF16).T
    return (pooled, grad_hidden, loss_value)


def solution(mesh, sizes=(4, 16, 4, 2)):
    mesh = Mesh(mesh.devices.reshape(sizes), ("x", "z", "y", "c"))
    both = P(("y", "c"), ("x", "z"))
    batch = P(("y", "c"))
    return jax.shard_map(
        local,
        mesh=mesh,
        in_specs=(both, both, both, batch, batch, batch, batch),
        out_specs=(both, both, P()),
        check_vma=False,
    )
```

```python
import functools
import math

import jax
import jax.numpy as jnp
from jax import lax
from jax.experimental import pallas as pl
from jax.experimental.pallas import tpu as pltpu
from jax.sharding import Mesh
from jax.sharding import PartitionSpec as P


VOCAB = 65536
QLEN = 16
LANES = 128
F32 = jnp.float32
BF16 = jnp.bfloat16


def ring(n, step):
    return [(i, (i + step) % n) for i in range(n)]


def spread(value, axes, n):
    return lax.all_to_all(jnp.broadcast_to(value[None], (n,) + value.shape), axes, 0, 0, tiled=True)


def dot(a, b, ca, cb):
    return lax.dot_general(a, b, (((ca,), (cb,)), ((), ())), preferred_element_type=F32)


ANY = pl.BlockSpec(memory_space=pl.ANY)
SMEM = pl.BlockSpec(memory_space=pltpu.SMEM)
WHOLE = pl.BlockSpec(memory_space=pltpu.VMEM)


def forward_kernel(nb, place, mine, theirs, *refs):
    blocks, (pooled, slope, feats, held, total, sems) = refs[:nb], refs[nb:]
    rows = held.shape[1]
    tok = mine.shape[1]
    copies = [
        pltpu.make_async_copy(mine, feats.at[:, pl.ds(0, tok)], sems.at[nb]),
        pltpu.make_async_copy(theirs, feats.at[:, pl.ds(tok, tok)], sems.at[nb + 1]),
    ]
    copies += [pltpu.make_async_copy(blocks[k], held.at[k], sems.at[k]) for k in range(nb)]
    for copy in copies:
        copy.start()
    copies[0].wait()
    copies[1].wait()
    for k in range(nb):
        copies[2 + k].wait()
        start = pl.multiple_of(place[k], rows)
        term = dot(feats[pl.ds(start, rows), :], held[k], 0, 0)
        if k:
            total[...] += term
        else:
            total[...] = term
    logits = total[...]
    positive = jnp.maximum(logits, 0.0)
    slope[...] = jnp.where(logits > 0, 1.0 / (1.0 + positive), 0.0)
    sums = jnp.log1p(positive).reshape(-1, QLEN, logits.shape[1]).sum(1)
    half = sums.shape[0] // 2
    first, second = sums[:half], sums[half:]
    swapped = place[nb] == 1
    pooled[:half, :] = jnp.where(swapped, second, first).astype(BF16)
    pooled[half:, :] = jnp.where(swapped, first, second).astype(BF16)


def forward(place, mine, theirs, blocks):
    nb, (rows, cols) = len(blocks), blocks[0].shape
    depth, tok = mine.shape
    queries = 2 * tok // QLEN
    return pl.pallas_call(
        functools.partial(forward_kernel, nb),
        name="forward",
        out_shape=(
            jax.ShapeDtypeStruct((queries, cols), BF16),
            jax.ShapeDtypeStruct((2 * tok, cols), F32),
        ),
        in_specs=[SMEM] + [ANY] * (2 + nb),
        out_specs=(WHOLE, WHOLE),
        scratch_shapes=[
            pltpu.VMEM((depth, 2 * tok), BF16),
            pltpu.VMEM((nb, rows, cols), BF16),
            pltpu.VMEM((2 * tok, cols), F32),
            pltpu.SemaphoreType.DMA((nb + 2,)),
        ],
        cost_estimate=pl.CostEstimate(
            flops=4 * tok * depth * cols,
            bytes_accessed=2 * depth * (2 * tok + cols) + 8 * tok * cols,
            transcendentals=2 * tok * cols,
        ),
        compiler_params=pltpu.CompilerParams(vmem_limit_bytes=32 << 20),
    )(place, mine, theirs, *blocks)


def backward_kernel(nb, place, grad, slope, *refs):
    blocks, (out, held, sems) = refs[:nb], refs[nb:]
    rows = held.shape[1]
    copies = [pltpu.make_async_copy(blocks[k], held.at[k], sems.at[k]) for k in range(nb)]
    for copy in copies:
        copy.start()
    tok, cols = slope.shape
    spread_grad = jnp.broadcast_to(grad[...][:, None, :], (tok // QLEN, QLEN, cols))
    logit_grad = (spread_grad.reshape(tok, cols) * slope[...]).astype(BF16)
    for k in range(nb):
        copies[k].wait()
        start = pl.multiple_of(place[k], rows)
        out[pl.ds(start, rows), :] = dot(held[k], logit_grad, 1, 1).astype(BF16)


def backward(place, grad, slope, blocks):
    nb, (rows, cols) = len(blocks), blocks[0].shape
    tok = slope.shape[0]
    depth = nb * rows
    return pl.pallas_call(
        functools.partial(backward_kernel, nb),
        name="backward",
        out_shape=jax.ShapeDtypeStruct((depth, tok), BF16),
        in_specs=[SMEM, WHOLE, WHOLE] + [ANY] * nb,
        out_specs=WHOLE,
        scratch_shapes=[
            pltpu.VMEM((nb, rows, cols), BF16),
            pltpu.SemaphoreType.DMA((nb,)),
        ],
        cost_estimate=pl.CostEstimate(
            flops=2 * tok * depth * cols,
            bytes_accessed=2 * depth * (tok + cols) + 4 * tok * cols,
            transcendentals=0,
        ),
        compiler_params=pltpu.CompilerParams(vmem_limit_bytes=32 << 20),
    )(place, grad, slope, *blocks)


def step(hidden, head, passages, pair_query, pair_passage, pair_count, teacher):
    nx, nz = lax.axis_size("x"), lax.axis_size("z")
    ny, nc = lax.axis_size("y"), lax.axis_size("c")
    y, c = lax.axis_index("y"), lax.axis_index("c")
    tok, feat = hidden.shape
    rows, cols = head.shape
    half = cols // nc
    batch = ny * nc
    queries = tok // QLEN
    swap = ring(nc, 1)
    plus, minus = ring(ny, 1), ring(ny, ny - 1)

    own = lax.dynamic_slice_in_dim(head, c * half, half, 1)
    sent = lax.dynamic_slice_in_dim(head, (1 - c) * half, half, 1)
    prev_own = lax.ppermute(own, "y", plus)
    next_own = lax.ppermute(own, "y", minus)
    pair = lax.ppermute(sent, "c", swap)
    next_pair = lax.ppermute(pair, "y", minus)
    prev_pair = lax.ppermute(pair, "y", plus)
    far_own = lax.ppermute(prev_own, "y", plus)
    far_pair = lax.ppermute(next_pair, "y", minus)

    part = spread(hidden.T, "z", nz).reshape(nz * feat, tok)
    mine = spread(part, "x", nx).reshape(nx * nz * feat, tok)
    theirs = lax.ppermute(mine, "c", swap)

    held = [
        (0, 0, own),
        (0, 1, pair),
        (ny - 1, 0, prev_own),
        (1, 0, next_own),
        (ny - 1, 1, prev_pair),
        (1, 1, next_pair),
        (2, 0, far_own),
        (2, 1, far_pair),
    ]
    blocks = [block for _, _, block in held]
    steps = jnp.array([step for step, _, _ in held], jnp.int32)
    others = jnp.array([other for _, other, _ in held], jnp.int32)
    owner = ((y + steps) % ny) * nc + (c + others) % nc
    place = jnp.concatenate([owner * rows, c[None]]).astype(jnp.int32)

    both, slope = forward(place, mine, theirs, blocks)
    every = spread(both, ("y", "c"), batch).reshape(ny, nc, nc * queries, half)
    halves = [every[:, i].reshape(batch * queries, half) for i in range(nc)]
    wide = jnp.concatenate(halves, axis=1)
    pooled = lax.dynamic_slice_in_dim(wide, (y * nc + c) * queries, queries, 0)

    inv_root = 1.0 / math.sqrt(VOCAB)
    slots = pair_query.shape[0]
    n_query, n_passage = batch * queries, passages.shape[0]
    table = dot(passages, wide, 1, 1)
    query_hot = (pair_query[None, :] == jnp.arange(n_query, dtype=jnp.int32)[:, None]).astype(F32)
    passage_hot = (
        pair_passage[None, :] == jnp.arange(n_passage, dtype=jnp.int32)[:, None]
    ).astype(F32)
    spread_table = jnp.dot(table, query_hot, precision=lax.Precision.HIGHEST)
    partial_value = (spread_table * passage_hot).sum(0)
    packed = jnp.pad(partial_value, (0, -slots % 512)).reshape(-1, LANES)
    packed = spread(packed, ("x", "z"), nx * nz).sum(0)
    scores = packed.reshape(-1)[:slots] * inv_root

    is_live = jnp.arange(slots, dtype=jnp.int32) < pair_count[0]
    residual = jnp.where(is_live, scores - teacher, 0.0)
    error = jnp.sum(residual * residual)
    pair_grad = 2.0 * residual * inv_root
    pair_table = lax.dot_general(
        query_hot,
        passage_hot * pair_grad[None, :],
        (((1,), (1,)), ((), ())),
        precision=lax.Precision.HIGHEST,
    )
    table_high = pair_table.astype(BF16)
    table_low = (pair_table - table_high.astype(F32)).astype(BF16)
    query_terms = dot(table_high, passages, 1, 0) + dot(table_low, passages, 1, 0)
    terms = jnp.stack(
        [
            query_terms[:, i * half : (i + 1) * half].reshape(ny, nc * queries, half)
            for i in range(nc)
        ],
        axis=1,
    ).reshape(batch, nc * queries, half)
    terms = jnp.concatenate(
        [terms, jnp.broadcast_to(error, (batch, nc * queries, LANES))], axis=2
    )
    terms = lax.all_to_all(terms, ("y", "c"), 0, 0, tiled=True).sum(0)
    loss_value = terms[0, half] / (slots * batch)
    grads = terms[:, :half].reshape(nc, queries, half)
    grad_mine = lax.dynamic_index_in_dim(grads, c, 0, keepdims=False)
    grad_theirs = lax.dynamic_index_in_dim(grads, 1 - c, 0, keepdims=False)

    terms_theirs = backward(place, grad_theirs, slope[tok:], blocks)
    terms_pair = lax.ppermute(terms_theirs, "c", swap)
    terms_mine = backward(place, grad_mine, slope[:tok], blocks)
    hidden_terms = (terms_mine.astype(F32) + terms_pair.astype(F32)).astype(BF16)
    hidden_terms = hidden_terms.reshape(nx, nz * feat, tok)
    over_x = lax.all_to_all(hidden_terms, "x", 0, 0, tiled=True)
    over_x = over_x.astype(F32).sum(0).astype(BF16).reshape(nz, feat, tok)
    over_z = lax.all_to_all(over_x, "z", 0, 0, tiled=True)
    grad_hidden = over_z.astype(F32).sum(0).astype(BF16).T
    return (pooled, grad_hidden, loss_value)


def solution(mesh, sizes=(4, 16, 4, 2)):
    mesh = Mesh(mesh.devices.reshape(sizes), ("x", "z", "y", "c"))
    both = P(("y", "c"), ("x", "z"))
    batch = P(("y", "c"))
    return jax.shard_map(
        step,
        mesh=mesh,
        in_specs=(both, both, both, batch, batch, batch, batch),
        out_specs=(both, both, P()),
        check_vma=False,
    )
```

```python
import functools
import math

import jax
import jax.numpy as jnp
from jax import lax
from jax.experimental import pallas as pl
from jax.experimental.pallas import tpu as pltpu
from jax.sharding import Mesh
from jax.sharding import PartitionSpec as P


VOCAB = 65536
QLEN = 16
LANES = 128
F32 = jnp.float32
BF16 = jnp.bfloat16


def ring(n, step):
    return [(i, (i + step) % n) for i in range(n)]


def spread(value, axes, n):
    return lax.all_to_all(jnp.broadcast_to(value[None], (n,) + value.shape), axes, 0, 0, tiled=True)


def dot(a, b, ca, cb):
    return lax.dot_general(a, b, (((ca,), (cb,)), ((), ())), preferred_element_type=F32)


ANY = pl.BlockSpec(memory_space=pl.ANY)
SMEM = pl.BlockSpec(memory_space=pltpu.SMEM)
WHOLE = pl.BlockSpec(memory_space=pltpu.VMEM)


def forward_kernel(nb, place, mine, theirs, *refs):
    blocks, (pooled, slope, feats, held, total, sems) = refs[:nb], refs[nb:]
    rows = held.shape[1]
    tok = mine.shape[1]
    copies = [
        pltpu.make_async_copy(mine, feats.at[:, pl.ds(0, tok)], sems.at[nb]),
        pltpu.make_async_copy(theirs, feats.at[:, pl.ds(tok, tok)], sems.at[nb + 1]),
    ]
    copies += [pltpu.make_async_copy(blocks[k], held.at[k], sems.at[k]) for k in range(nb)]
    for copy in copies:
        copy.start()
    copies[0].wait()
    copies[1].wait()
    for k in range(nb):
        copies[2 + k].wait()
        start = pl.multiple_of(place[k], rows)
        term = dot(feats[pl.ds(start, rows), :], held[k], 0, 0)
        if k:
            total[...] += term
        else:
            total[...] = term
    logits = total[...]
    positive = jnp.maximum(logits, 0.0)
    slope[...] = jnp.where(logits > 0, 1.0 / (1.0 + positive), 0.0)
    sums = jnp.log1p(positive).reshape(-1, QLEN, logits.shape[1]).sum(1)
    half = sums.shape[0] // 2
    first, second = sums[:half], sums[half:]
    swapped = place[nb] == 1
    pooled[:half, :] = jnp.where(swapped, second, first).astype(BF16)
    pooled[half:, :] = jnp.where(swapped, first, second).astype(BF16)


def forward(place, mine, theirs, blocks):
    nb, (rows, cols) = len(blocks), blocks[0].shape
    depth, tok = mine.shape
    queries = 2 * tok // QLEN
    return pl.pallas_call(
        functools.partial(forward_kernel, nb),
        name="forward",
        out_shape=(
            jax.ShapeDtypeStruct((queries, cols), BF16),
            jax.ShapeDtypeStruct((2 * tok, cols), F32),
        ),
        in_specs=[SMEM] + [ANY] * (2 + nb),
        out_specs=(WHOLE, WHOLE),
        scratch_shapes=[
            pltpu.VMEM((depth, 2 * tok), BF16),
            pltpu.VMEM((nb, rows, cols), BF16),
            pltpu.VMEM((2 * tok, cols), F32),
            pltpu.SemaphoreType.DMA((nb + 2,)),
        ],
        cost_estimate=pl.CostEstimate(
            flops=4 * tok * depth * cols,
            bytes_accessed=2 * depth * (2 * tok + cols) + 8 * tok * cols,
            transcendentals=2 * tok * cols,
        ),
        compiler_params=pltpu.CompilerParams(vmem_limit_bytes=32 << 20),
    )(place, mine, theirs, *blocks)


def scores_kernel(place, every, passages, pair_query, pair_passage, out, pooled):
    groups, queries, half = every.shape
    cores = passages.shape[1] // half
    c, y = place[place.shape[0] - 2], place[place.shape[0] - 1]
    table = None
    for i in range(cores):
        columns = pl.ds(i * half, half)
        part = jnp.concatenate([every[g] for g in range(i, groups, cores)], axis=0)
        term = dot(passages[:, columns], part, 1, 1)
        table = term if table is None else table + term
        here = every[y * cores + i].astype(F32)
        kept = queries // cores
        pooled[:, columns] = jnp.where(c == 1, here[kept:], here[:kept]).astype(BF16)
    n_passage, n_query = table.shape
    slots = pair_query.shape[1]
    query_hot = pair_query[...] == lax.broadcasted_iota(jnp.int32, (n_query, slots), 0)
    passage_hot = pair_passage[...] == lax.broadcasted_iota(jnp.int32, (n_passage, slots), 0)
    spread_table = lax.dot_general(
        table,
        query_hot.astype(F32),
        (((1,), (0,)), ((), ())),
        precision=lax.Precision.HIGHEST,
        preferred_element_type=F32,
    )
    value = jnp.where(passage_hot, spread_table, 0.0).sum(0, keepdims=True)
    out[...] = jnp.broadcast_to(value[None], out.shape)


def pair_scores(place, every, passages, pair_query, pair_passage, peers):
    slots = pair_query.shape[1]
    _, queries, half = every.shape
    cores = passages.shape[1] // half
    return pl.pallas_call(
        scores_kernel,
        name="pair_scores",
        out_shape=(
            jax.ShapeDtypeStruct((peers, 1, slots), F32),
            jax.ShapeDtypeStruct((queries // cores, cores * half), BF16),
        ),
        in_specs=[SMEM] + [WHOLE] * 4,
        out_specs=(WHOLE, WHOLE),
        compiler_params=pltpu.CompilerParams(vmem_limit_bytes=16 << 20),
    )(place, every, passages, pair_query, pair_passage)


def terms_kernel(pair_count, partials, teacher, pair_query, pair_passage, passages, out):
    groups, queries, width = out.shape
    half = width - LANES
    cores = passages.shape[1] // half
    slots = pair_query.shape[1]
    inv_root = 1.0 / math.sqrt(VOCAB)
    scores = partials[...].sum(0) * inv_root
    is_live = lax.broadcasted_iota(jnp.int32, (1, slots), 1) < pair_count[0]
    residual = jnp.where(is_live, scores - teacher[...], 0.0)
    error = jnp.sum(residual * residual)
    pair_grad = 2.0 * residual * inv_root
    n_query, n_passage = queries * groups // cores, passages.shape[0]
    query_hot = pair_query[...] == lax.broadcasted_iota(jnp.int32, (n_query, slots), 0)
    passage_hot = pair_passage[...] == lax.broadcasted_iota(jnp.int32, (n_passage, slots), 0)
    table = lax.dot_general(
        query_hot.astype(F32),
        jnp.where(passage_hot, pair_grad, 0.0),
        (((1,), (1,)), ((), ())),
        precision=lax.Precision.HIGHEST,
        preferred_element_type=F32,
    )
    high = table.astype(BF16)
    low = (table - high.astype(F32)).astype(BF16)
    parts = jnp.concatenate([high, low], axis=0)
    for i in range(cores):
        both = dot(parts, passages[:, i * half : (i + 1) * half], 1, 0)
        terms = both[:n_query] + both[n_query:]
        for k in range(groups // cores):
            out[k * cores + i, :, :half] = terms[k * queries : (k + 1) * queries]
    out[:, :, half:] = jnp.full((groups, queries, LANES), error, F32)


def query_terms(pair_count, partials, teacher, pair_query, pair_passage, passages, shape):
    return pl.pallas_call(
        terms_kernel,
        name="query_terms",
        out_shape=jax.ShapeDtypeStruct(shape, F32),
        in_specs=[SMEM] + [WHOLE] * 5,
        out_specs=WHOLE,
        compiler_params=pltpu.CompilerParams(vmem_limit_bytes=16 << 20),
    )(pair_count, partials, teacher, pair_query, pair_passage, passages)


PARTS = 2


def multiply(place, part, blocks, held, sems, logit_grad, mine, theirs):
    nb = len(blocks)
    rows = held.shape[1] * held.shape[2]
    tok = mine.shape[1]
    for k in range(nb):
        pltpu.make_async_copy(blocks[k].at[:, part], held.at[k], sems.at[k]).wait()
        start = pl.multiple_of(place[k] // PARTS, rows)
        block = held[k].reshape(rows, held.shape[3])
        term = dot(block, logit_grad, 1, 1).astype(BF16)
        mine[pl.ds(start, rows), :] = term[:, :tok]
        theirs[pl.ds(start, rows), :] = term[:, tok:]


def first_kernel(nb, place, terms, slope, *refs):
    blocks, (mine, theirs, grads, loss, held, sems) = refs[:nb], refs[nb:]
    for k in range(nb):
        pltpu.make_async_copy(blocks[k].at[:, 0], held.at[k], sems.at[k]).start()
    tok, cols = slope.shape
    total = terms[...].sum(0)
    loss[...] = total[:1, cols:]
    half = total.shape[0] // 2
    swapped = place[nb] == 1
    one, two = total[:half, :cols], total[half:, :cols]
    kept = jnp.concatenate([jnp.where(swapped, two, one), jnp.where(swapped, one, two)], axis=0)
    wide = jnp.broadcast_to(kept[:, None, :], (tok // QLEN, QLEN, cols)).reshape(tok, cols)
    grads[...] = (wide * slope[...]).astype(BF16)
    multiply(place, 0, blocks, held, sems, grads[...], mine, theirs)


def next_kernel(nb, part, place, grads, *refs):
    blocks, (mine, theirs, held, sems) = refs[:nb], refs[nb:]
    for k in range(nb):
        pltpu.make_async_copy(blocks[k].at[:, part], held.at[k], sems.at[k]).start()
    multiply(place, part, blocks, held, sems, grads[...], mine, theirs)


def backward_call(part, place, given, blocks):
    nb = len(blocks)
    lead, _, rows, cols = blocks[0].shape
    tok = given[-1].shape[0] // 2
    depth = nb * lead * rows
    shapes = [jax.ShapeDtypeStruct((depth, tok), BF16)] * 2
    if part == 0:
        shapes += [
            jax.ShapeDtypeStruct((2 * tok, cols), BF16),
            jax.ShapeDtypeStruct((1, LANES), F32),
        ]
    body = functools.partial(first_kernel, nb)
    if part:
        body = functools.partial(next_kernel, nb, part)
    return pl.pallas_call(
        body,
        out_shape=tuple(shapes),
        in_specs=[SMEM] + [WHOLE] * len(given) + [ANY] * nb,
        out_specs=(WHOLE,) * len(shapes),
        scratch_shapes=[
            pltpu.VMEM((nb, lead, rows, cols), BF16),
            pltpu.SemaphoreType.DMA((nb,)),
        ],
        cost_estimate=pl.CostEstimate(
            flops=4 * tok * depth * cols,
            bytes_accessed=2 * depth * (2 * tok + cols) + 4 * tok * cols,
            transcendentals=0,
        ),
        compiler_params=pltpu.CompilerParams(vmem_limit_bytes=32 << 20),
    )(place, *given, *blocks)


def step(hidden, head, passages, pair_query, pair_passage, pair_count, teacher):
    nx, nz = lax.axis_size("x"), lax.axis_size("z")
    ny, nc = lax.axis_size("y"), lax.axis_size("c")
    y, c = lax.axis_index("y"), lax.axis_index("c")
    tok, feat = hidden.shape
    rows, cols = head.shape
    half = cols // nc
    batch = ny * nc
    queries = tok // QLEN
    swap = ring(nc, 1)
    plus, minus = ring(ny, 1), ring(ny, ny - 1)

    own = lax.dynamic_slice_in_dim(head, c * half, half, 1)
    sent = lax.dynamic_slice_in_dim(head, (1 - c) * half, half, 1)
    prev_own = lax.ppermute(own, "y", plus)
    next_own = lax.ppermute(own, "y", minus)
    pair = lax.ppermute(sent, "c", swap)
    next_pair = lax.ppermute(pair, "y", minus)
    prev_pair = lax.ppermute(pair, "y", plus)
    far_own = lax.ppermute(prev_own, "y", plus)
    far_pair = lax.ppermute(next_pair, "y", minus)

    part = spread(hidden.T, "z", nz).reshape(nz * feat, tok)
    mine = spread(part, "x", nx).reshape(nx * nz * feat, tok)
    theirs = lax.ppermute(mine, "c", swap)

    held = [
        (0, 0, own),
        (0, 1, pair),
        (ny - 1, 0, prev_own),
        (1, 0, next_own),
        (ny - 1, 1, prev_pair),
        (1, 1, next_pair),
        (2, 0, far_own),
        (2, 1, far_pair),
    ]
    blocks = [block for _, _, block in held]
    steps = jnp.array([step for step, _, _ in held], jnp.int32)
    others = jnp.array([other for _, other, _ in held], jnp.int32)
    owner = ((y + steps) % ny) * nc + (c + others) % nc
    place = jnp.concatenate([owner * rows, c[None], y[None]]).astype(jnp.int32)

    both, slope = forward(place, mine, theirs, blocks)
    every = spread(both, ("y", "c"), batch)

    slots = pair_query.shape[0]
    pair_query, pair_passage = pair_query.reshape(1, slots), pair_passage.reshape(1, slots)
    partials, pooled = pair_scores(place, every, passages, pair_query, pair_passage, nx * nz)
    partials = lax.all_to_all(partials, ("x", "z"), 0, 0, tiled=True)
    terms = query_terms(
        pair_count,
        partials,
        teacher.reshape(1, slots),
        pair_query,
        pair_passage,
        passages,
        (batch, nc * queries, half + LANES),
    )
    terms = lax.all_to_all(terms, ("y", "c"), 0, 0, tiled=True)

    sliced = [block.reshape(rows // feat, PARTS, feat // PARTS, half) for block in blocks]
    given = (terms, slope)
    sums = []
    for part in range(PARTS):
        results = backward_call(part, place, given, sliced)
        if part == 0:
            given = (results[2],)
            loss_value = results[3][0, 0] / (slots * batch)
        other = lax.ppermute(results[1], "c", swap)
        sums.append((results[0], other))
    slices = []
    for part, (kept, other) in enumerate(sums):
        shape = (nx, nz * feat // PARTS, tok)
        hidden_terms = (kept.astype(F32) + other.astype(F32)).astype(BF16).reshape(shape)
        over_x = lax.all_to_all(hidden_terms, "x", 0, 0, tiled=True)
        over_x = over_x.astype(F32).sum(0).astype(BF16).reshape(nz, feat // PARTS, tok)
        over_z = lax.all_to_all(over_x, "z", 0, 0, tiled=True)
        slices.append(over_z.astype(F32).sum(0).astype(BF16))
    grad_hidden = jnp.concatenate(slices, axis=0).T
    return (pooled, grad_hidden, loss_value)


def solution(mesh, sizes=(4, 16, 4, 2)):
    mesh = Mesh(mesh.devices.reshape(sizes), ("x", "z", "y", "c"))
    both = P(("y", "c"), ("x", "z"))
    batch = P(("y", "c"))
    return jax.shard_map(
        step,
        mesh=mesh,
        in_specs=(both, both, both, batch, batch, batch, batch),
        out_specs=(both, both, P()),
        check_vma=False,
    )
```

```python
import functools
import math

import jax
import jax.numpy as jnp
from jax import lax
from jax.experimental import pallas as pl
from jax.experimental.pallas import tpu as pltpu
from jax.sharding import Mesh
from jax.sharding import PartitionSpec as P


VOCAB = 65536
QLEN = 16
LANES = 128
F32 = jnp.float32
BF16 = jnp.bfloat16


def ring(n, step):
    return [(i, (i + step) % n) for i in range(n)]


def spread(value, axes, n):
    return lax.all_to_all(jnp.broadcast_to(value[None], (n,) + value.shape), axes, 0, 0, tiled=True)


def dot(a, b, ca, cb):
    return lax.dot_general(a, b, (((ca,), (cb,)), ((), ())), preferred_element_type=F32)


ANY = pl.BlockSpec(memory_space=pl.ANY)
SMEM = pl.BlockSpec(memory_space=pltpu.SMEM)
WHOLE = pl.BlockSpec(memory_space=pltpu.VMEM)


def forward_kernel(nb, place, mine, theirs, *refs):
    blocks, (pooled, total, feats, held, sems) = refs[:nb], refs[nb:]
    rows = held.shape[1]
    tok = mine.shape[1]
    copies = [
        pltpu.make_async_copy(mine, feats.at[:, pl.ds(0, tok)], sems.at[nb]),
        pltpu.make_async_copy(theirs, feats.at[:, pl.ds(tok, tok)], sems.at[nb + 1]),
    ]
    copies += [pltpu.make_async_copy(blocks[k], held.at[k], sems.at[k]) for k in range(nb)]
    for copy in copies:
        copy.start()
    copies[0].wait()
    copies[1].wait()
    for k in range(nb):
        copies[2 + k].wait()
        start = pl.multiple_of(place[k], rows)
        term = dot(feats[pl.ds(start, rows), :], held[k], 0, 0)
        if k:
            total[...] += term
        else:
            total[...] = term
    sums = jnp.log1p(jnp.maximum(total[...], 0.0)).reshape(-1, QLEN, total.shape[1]).sum(1)
    half = sums.shape[0] // 2
    first, second = sums[:half], sums[half:]
    swapped = place[nb] == 1
    pooled[:half, :] = jnp.where(swapped, second, first).astype(BF16)
    pooled[half:, :] = jnp.where(swapped, first, second).astype(BF16)


def forward(place, mine, theirs, blocks):
    nb, (rows, cols) = len(blocks), blocks[0].shape
    depth, tok = mine.shape
    queries = 2 * tok // QLEN
    return pl.pallas_call(
        functools.partial(forward_kernel, nb),
        name="forward",
        out_shape=(
            jax.ShapeDtypeStruct((queries, cols), BF16),
            jax.ShapeDtypeStruct((2 * tok, cols), F32),
        ),
        in_specs=[SMEM] + [ANY] * (2 + nb),
        out_specs=(WHOLE, WHOLE),
        scratch_shapes=[
            pltpu.VMEM((depth, 2 * tok), BF16),
            pltpu.VMEM((nb, rows, cols), BF16),
            pltpu.SemaphoreType.DMA((nb + 2,)),
        ],
        cost_estimate=pl.CostEstimate(
            flops=4 * tok * depth * cols,
            bytes_accessed=2 * depth * (2 * tok + cols) + 8 * tok * cols,
            transcendentals=2 * tok * cols,
        ),
        compiler_params=pltpu.CompilerParams(vmem_limit_bytes=32 << 20),
    )(place, mine, theirs, *blocks)


def terms_kernel(
    pair_count, partials, teacher, pair_query, pair_passage, stored, out, passages, sem
):
    copy = pltpu.make_async_copy(stored, passages, sem)
    copy.start()
    groups, queries, width = out.shape
    half = width - LANES
    cores = passages.shape[1] // half
    slots = pair_query.shape[1]
    inv_root = 1.0 / math.sqrt(VOCAB)
    total = partials[...].sum(0)
    lines = slots // LANES
    scores = jnp.concatenate([total[i : i + 1] for i in range(lines)], axis=1) * inv_root
    is_live = lax.broadcasted_iota(jnp.int32, (1, slots), 1) < pair_count[0]
    residual = jnp.where(is_live, scores - teacher[...], 0.0)
    error = jnp.sum(residual * residual)
    pair_grad = 2.0 * residual * inv_root
    n_query, n_passage = queries * groups // cores, passages.shape[0]
    query_hot = pair_query[...] == lax.broadcasted_iota(jnp.int32, (n_query, slots), 0)
    passage_hot = pair_passage[...] == lax.broadcasted_iota(jnp.int32, (n_passage, slots), 0)
    table = lax.dot_general(
        query_hot.astype(F32),
        jnp.where(passage_hot, pair_grad, 0.0),
        (((1,), (1,)), ((), ())),
        precision=lax.Precision.HIGHEST,
        preferred_element_type=F32,
    )
    high = table.astype(BF16)
    low = (table - high.astype(F32)).astype(BF16)
    parts = jnp.concatenate([high, low], axis=0)
    copy.wait()
    for i in range(cores):
        both = dot(parts, passages[:, i * half : (i + 1) * half], 1, 0)
        terms = both[:n_query] + both[n_query:]
        for k in range(groups // cores):
            out[k * cores + i, :, :half] = terms[k * queries : (k + 1) * queries]
    out[:, :, half:] = jnp.full((groups, queries, LANES), error, F32)


def query_terms(pair_count, partials, teacher, pair_query, pair_passage, passages, shape):
    return pl.pallas_call(
        terms_kernel,
        name="query_terms",
        out_shape=jax.ShapeDtypeStruct(shape, F32),
        in_specs=[SMEM] + [WHOLE] * 4 + [ANY],
        out_specs=WHOLE,
        scratch_shapes=[pltpu.VMEM(passages.shape, BF16), pltpu.SemaphoreType.DMA(())],
        compiler_params=pltpu.CompilerParams(vmem_limit_bytes=16 << 20),
    )(pair_count, partials, teacher, pair_query, pair_passage, passages)


def backward_kernel(nb, place, terms, slope, *refs):
    blocks, (mine, theirs, loss, held, sems) = refs[:nb], refs[nb:]
    rows = blocks[0].shape[0]
    tok, cols = slope.shape
    copies = []
    for k in range(nb):
        start = pl.multiple_of(place[k], rows)
        copies.append(pltpu.make_async_copy(blocks[k], held.at[pl.ds(start, rows)], sems.at[k]))
        copies[k].start()
    total = terms[...].sum(0)
    loss[...] = total[:1, cols:]
    half = total.shape[0] // 2
    swapped = place[nb] == 1
    one, two = total[:half, :cols], total[half:, :cols]
    kept = jnp.concatenate([jnp.where(swapped, two, one), jnp.where(swapped, one, two)], axis=0)
    wide = jnp.broadcast_to(kept[:, None, :], (tok // QLEN, QLEN, cols)).reshape(tok, cols)
    logit_grad = (wide * slope[...]).astype(BF16)
    for copy in copies:
        copy.wait()
    step = 2 * rows
    for start in range(0, nb * rows, step):
        term = dot(held[start : start + step, :], logit_grad, 1, 1).astype(BF16)
        mine[start : start + step, :] = term[:, : tok // 2]
        theirs[start : start + step, :] = term[:, tok // 2 :]


def backward(place, terms, slope, blocks):
    nb, (rows, cols) = len(blocks), blocks[0].shape
    tok = slope.shape[0]
    depth = nb * rows
    return pl.pallas_call(
        functools.partial(backward_kernel, nb),
        name="backward",
        out_shape=(
            jax.ShapeDtypeStruct((depth, tok // 2), BF16),
            jax.ShapeDtypeStruct((depth, tok // 2), BF16),
            jax.ShapeDtypeStruct((1, LANES), F32),
        ),
        in_specs=[SMEM, WHOLE, WHOLE] + [ANY] * nb,
        out_specs=(WHOLE,) * 3,
        scratch_shapes=[
            pltpu.VMEM((depth, cols), BF16),
            pltpu.SemaphoreType.DMA((nb,)),
        ],
        cost_estimate=pl.CostEstimate(
            flops=2 * tok * depth * cols,
            bytes_accessed=2 * depth * (tok + cols) + 4 * tok * cols,
            transcendentals=0,
        ),
        compiler_params=pltpu.CompilerParams(vmem_limit_bytes=32 << 20),
    )(place, terms, slope, *blocks)


def step(hidden, head, passages, pair_query, pair_passage, pair_count, teacher):
    nx, nz = lax.axis_size("x"), lax.axis_size("z")
    ny, nc = lax.axis_size("y"), lax.axis_size("c")
    y, c = lax.axis_index("y"), lax.axis_index("c")
    tok, feat = hidden.shape
    rows, cols = head.shape
    half = cols // nc
    batch = ny * nc
    queries = tok // QLEN
    swap = ring(nc, 1)
    plus, minus = ring(ny, 1), ring(ny, ny - 1)

    own = lax.dynamic_slice_in_dim(head, c * half, half, 1)
    sent = lax.dynamic_slice_in_dim(head, (1 - c) * half, half, 1)
    prev_own = lax.ppermute(own, "y", plus)
    next_own = lax.ppermute(own, "y", minus)
    pair = lax.ppermute(sent, "c", swap)
    next_pair = lax.ppermute(pair, "y", minus)
    prev_pair = lax.ppermute(pair, "y", plus)
    far_own = lax.ppermute(prev_own, "y", plus)
    far_pair = lax.ppermute(next_pair, "y", minus)

    part = spread(hidden.T, "z", nz).reshape(nz * feat, tok)
    mine = spread(part, "x", nx).reshape(nx * nz * feat, tok)
    theirs = lax.ppermute(mine, "c", swap)

    held = [
        (0, 0, own),
        (0, 1, pair),
        (ny - 1, 0, prev_own),
        (1, 0, next_own),
        (ny - 1, 1, prev_pair),
        (1, 1, next_pair),
        (2, 0, far_own),
        (2, 1, far_pair),
    ]
    blocks = [block for _, _, block in held]
    steps = jnp.array([step for step, _, _ in held], jnp.int32)
    others = jnp.array([other for _, other, _ in held], jnp.int32)
    owner = ((y + steps) % ny) * nc + (c + others) % nc
    place = jnp.concatenate([owner * rows, c[None], y[None]]).astype(jnp.int32)

    both, logits = forward(place, mine, theirs, blocks)
    every = spread(both, ("y", "c"), batch).reshape(ny, nc, nc * queries, half)
    halves = [every[:, i].reshape(batch * queries, half) for i in range(nc)]
    wide = jnp.concatenate(halves, axis=1)
    pooled = lax.dynamic_slice_in_dim(wide, (y * nc + c) * queries, queries, 0)

    slots = pair_query.shape[0]
    n_query, n_passage = batch * queries, passages.shape[0]
    pair_query, pair_passage = pair_query.reshape(1, slots), pair_passage.reshape(1, slots)
    table = dot(passages, wide, 1, 1)
    query_hot = (pair_query == jnp.arange(n_query, dtype=jnp.int32)[:, None]).astype(F32)
    passage_hot = (pair_passage == jnp.arange(n_passage, dtype=jnp.int32)[:, None]).astype(F32)
    spread_table = jnp.dot(table, query_hot, precision=lax.Precision.HIGHEST)
    partial_value = (spread_table * passage_hot).sum(0)
    packed = jnp.pad(partial_value, (0, -slots % 512)).reshape(-1, LANES)
    partials = spread(packed, ("x", "z"), nx * nz)
    positive = jnp.maximum(logits, 0.0)
    slope = jnp.where(logits > 0, 1.0 / (1.0 + positive), 0.0)

    terms = query_terms(
        pair_count,
        partials,
        teacher.reshape(1, slots),
        pair_query,
        pair_passage,
        passages,
        (batch, nc * queries, half + LANES),
    )
    terms = lax.all_to_all(terms, ("y", "c"), 0, 0, tiled=True)

    kept, sent, loss = backward(place, terms, slope, blocks)
    loss_value = loss[0, 0] / (slots * batch)
    other = lax.ppermute(sent, "c", swap)
    hidden_terms = (kept.astype(F32) + other.astype(F32)).astype(BF16)
    hidden_terms = hidden_terms.reshape(nx, nz * feat, tok)
    over_x = lax.all_to_all(hidden_terms, "x", 0, 0, tiled=True)
    over_x = over_x.astype(F32).sum(0).astype(BF16).reshape(nz, feat, tok)
    over_z = lax.all_to_all(over_x, "z", 0, 0, tiled=True)
    grad_hidden = over_z.astype(F32).sum(0).astype(BF16).T
    return (pooled, grad_hidden, loss_value)


def solution(mesh, sizes=(4, 16, 4, 2)):
    mesh = Mesh(mesh.devices.reshape(sizes), ("x", "z", "y", "c"))
    both = P(("y", "c"), ("x", "z"))
    batch = P(("y", "c"))
    return jax.shard_map(
        step,
        mesh=mesh,
        in_specs=(both, both, both, batch, batch, batch, batch),
        out_specs=(both, both, P()),
        check_vma=False,
    )
```

```python
import functools
import math

import jax
import jax.numpy as jnp
from jax import lax
from jax.experimental import pallas as pl
from jax.experimental.pallas import tpu as pltpu
from jax.sharding import Mesh
from jax.sharding import PartitionSpec as P


VOCAB = 65536
QLEN = 16
LANES = 128
F32 = jnp.float32
BF16 = jnp.bfloat16


def ring(n, step):
    return [(i, (i + step) % n) for i in range(n)]


def cross(ny, nc, step):
    return [
        (y * nc + c, ((y + step) % ny) * nc + (c + 1) % nc) for y in range(ny) for c in range(nc)
    ]


def spread(value, axes, n):
    return lax.all_to_all(jnp.broadcast_to(value[None], (n,) + value.shape), axes, 0, 0, tiled=True)


def dot(a, b, ca, cb):
    return lax.dot_general(a, b, (((ca,), (cb,)), ((), ())), preferred_element_type=F32)


ANY = pl.BlockSpec(memory_space=pl.ANY)
SMEM = pl.BlockSpec(memory_space=pltpu.SMEM)
WHOLE = pl.BlockSpec(memory_space=pltpu.VMEM)


def forward_kernel(nb, place, mine, theirs, *refs):
    blocks, (pooled, logits, feats, held, total, sems) = refs[:nb], refs[nb:]
    rows = held.shape[1]
    tok = mine.shape[1]
    copies = [
        pltpu.make_async_copy(mine, feats.at[:, pl.ds(0, tok)], sems.at[nb]),
        pltpu.make_async_copy(theirs, feats.at[:, pl.ds(tok, tok)], sems.at[nb + 1]),
    ]
    copies += [pltpu.make_async_copy(blocks[k], held.at[k], sems.at[k]) for k in range(nb)]
    for copy in copies:
        copy.start()
    copies[0].wait()
    copies[1].wait()
    for k in range(nb):
        copies[2 + k].wait()
        start = pl.multiple_of(place[k], rows)
        term = dot(feats[pl.ds(start, rows), :], held[k], 0, 0)
        if k:
            total[...] += term
        else:
            total[...] = term
    keep = pltpu.make_async_copy(total, logits, sems.at[nb + 2])
    keep.start()
    sums = jnp.log1p(jnp.maximum(total[...], 0.0)).reshape(-1, QLEN, total.shape[1]).sum(1)
    half = sums.shape[0] // 2
    first, second = sums[:half], sums[half:]
    swapped = place[nb] == 1
    pooled[:half, :] = jnp.where(swapped, second, first).astype(BF16)
    pooled[half:, :] = jnp.where(swapped, first, second).astype(BF16)
    keep.wait()


def forward(place, mine, theirs, blocks):
    nb, (rows, cols) = len(blocks), blocks[0].shape
    depth, tok = mine.shape
    queries = 2 * tok // QLEN
    return pl.pallas_call(
        functools.partial(forward_kernel, nb),
        name="forward",
        out_shape=(
            jax.ShapeDtypeStruct((queries, cols), BF16),
            jax.ShapeDtypeStruct((2 * tok, cols), F32),
        ),
        in_specs=[SMEM] + [ANY] * (2 + nb),
        out_specs=(WHOLE, ANY),
        scratch_shapes=[
            pltpu.VMEM((depth, 2 * tok), BF16),
            pltpu.VMEM((nb, rows, cols), BF16),
            pltpu.VMEM((2 * tok, cols), F32),
            pltpu.SemaphoreType.DMA((nb + 3,)),
        ],
        cost_estimate=pl.CostEstimate(
            flops=4 * tok * depth * cols,
            bytes_accessed=2 * depth * (2 * tok + cols) + 8 * tok * cols,
            transcendentals=2 * tok * cols,
        ),
        compiler_params=pltpu.CompilerParams(vmem_limit_bytes=32 << 20),
    )(place, mine, theirs, *blocks)


def terms_kernel(
    pair_count, partials, teacher, pair_query, pair_passage, stored, out, passages, sem
):
    copy = pltpu.make_async_copy(stored, passages, sem)
    copy.start()
    groups, queries, width = out.shape
    half = width - LANES
    cores = passages.shape[1] // half
    slots = pair_query.shape[1]
    inv_root = 1.0 / math.sqrt(VOCAB)
    total = partials[...].sum(0)
    lines = slots // LANES
    scores = jnp.concatenate([total[i : i + 1] for i in range(lines)], axis=1) * inv_root
    is_live = lax.broadcasted_iota(jnp.int32, (1, slots), 1) < pair_count[0]
    residual = jnp.where(is_live, scores - teacher[...], 0.0)
    error = jnp.sum(residual * residual)
    pair_grad = 2.0 * residual * inv_root
    n_query, n_passage = queries * groups // cores, passages.shape[0]
    query_hot = pair_query[...] == lax.broadcasted_iota(jnp.int32, (n_query, slots), 0)
    passage_hot = pair_passage[...] == lax.broadcasted_iota(jnp.int32, (n_passage, slots), 0)
    table = lax.dot_general(
        query_hot.astype(F32),
        jnp.where(passage_hot, pair_grad, 0.0),
        (((1,), (1,)), ((), ())),
        precision=lax.Precision.HIGHEST,
        preferred_element_type=F32,
    )
    high = table.astype(BF16)
    low = (table - high.astype(F32)).astype(BF16)
    parts = jnp.concatenate([high, low], axis=0)
    copy.wait()
    for i in range(cores):
        both = dot(parts, passages[:, i * half : (i + 1) * half], 1, 0)
        terms = both[:n_query] + both[n_query:]
        for k in range(groups // cores):
            out[k * cores + i, :, :half] = terms[k * queries : (k + 1) * queries].astype(BF16)
    errors = jnp.full((groups, queries, LANES), error, F32)
    error_high = errors.astype(BF16)
    error_low = (errors - error_high.astype(F32)).astype(BF16)
    lane = lax.broadcasted_iota(jnp.int32, errors.shape, 2)
    out[:, :, half:] = jnp.where(lane < LANES // 2, error_high, error_low)


def query_terms(pair_count, partials, teacher, pair_query, pair_passage, passages, shape):
    return pl.pallas_call(
        terms_kernel,
        name="query_terms",
        out_shape=jax.ShapeDtypeStruct(shape, BF16),
        in_specs=[SMEM] + [WHOLE] * 4 + [ANY],
        out_specs=WHOLE,
        scratch_shapes=[pltpu.VMEM(passages.shape, BF16), pltpu.SemaphoreType.DMA(())],
        compiler_params=pltpu.CompilerParams(vmem_limit_bytes=16 << 20),
    )(pair_count, partials, teacher, pair_query, pair_passage, passages)


def backward_kernel(nb, place, terms, slope, *refs):
    blocks, (mine, theirs, loss, held, sems) = refs[:nb], refs[nb:]
    rows = blocks[0].shape[0]
    tok, cols = slope.shape
    copies = []
    for k in range(nb):
        start = pl.multiple_of(place[k], rows)
        copies.append(pltpu.make_async_copy(blocks[k], held.at[pl.ds(start, rows)], sems.at[k]))
        copies[k].start()
    total = terms[...].astype(F32).sum(0)
    loss[...] = total[:1, cols:]
    half = total.shape[0] // 2
    swapped = place[nb] == 1
    one, two = total[:half, :cols], total[half:, :cols]
    kept = jnp.concatenate([jnp.where(swapped, two, one), jnp.where(swapped, one, two)], axis=0)
    wide = jnp.broadcast_to(kept[:, None, :], (tok // QLEN, QLEN, cols)).reshape(tok, cols)
    logit_grad = (wide * slope[...]).astype(BF16)
    for copy in copies:
        copy.wait()
    step = 2 * rows
    for start in range(0, nb * rows, step):
        term = dot(held[start : start + step, :], logit_grad, 1, 1).astype(BF16)
        mine[start : start + step, :] = term[:, : tok // 2]
        theirs[start : start + step, :] = term[:, tok // 2 :]


def backward(place, terms, slope, blocks):
    nb, (rows, cols) = len(blocks), blocks[0].shape
    tok = slope.shape[0]
    depth = nb * rows
    return pl.pallas_call(
        functools.partial(backward_kernel, nb),
        name="backward",
        out_shape=(
            jax.ShapeDtypeStruct((depth, tok // 2), BF16),
            jax.ShapeDtypeStruct((depth, tok // 2), BF16),
            jax.ShapeDtypeStruct((1, LANES), F32),
        ),
        in_specs=[SMEM, WHOLE, WHOLE] + [ANY] * nb,
        out_specs=(WHOLE,) * 3,
        scratch_shapes=[
            pltpu.VMEM((depth, cols), BF16),
            pltpu.SemaphoreType.DMA((nb,)),
        ],
        cost_estimate=pl.CostEstimate(
            flops=2 * tok * depth * cols,
            bytes_accessed=2 * depth * (tok + cols) + 4 * tok * cols,
            transcendentals=0,
        ),
        compiler_params=pltpu.CompilerParams(vmem_limit_bytes=32 << 20),
    )(place, terms, slope, *blocks)


def step(hidden, head, passages, pair_query, pair_passage, pair_count, teacher):
    nx, nz = lax.axis_size("x"), lax.axis_size("z")
    ny, nc = lax.axis_size("y"), lax.axis_size("c")
    y, c = lax.axis_index("y"), lax.axis_index("c")
    tok, feat = hidden.shape
    rows, cols = head.shape
    half = cols // nc
    batch = ny * nc
    queries = tok // QLEN
    swap = ring(nc, 1)
    plus, minus = ring(ny, 1), ring(ny, ny - 1)

    own = lax.dynamic_slice_in_dim(head, c * half, half, 1)
    sent = lax.dynamic_slice_in_dim(head, (1 - c) * half, half, 1)
    cross_plus, cross_minus = cross(ny, nc, 1), cross(ny, nc, ny - 1)
    next_pair = lax.ppermute(sent, ("y", "c"), cross_minus)
    prev_own = lax.ppermute(own, "y", plus)
    next_own = lax.ppermute(own, "y", minus)
    prev_pair = lax.ppermute(sent, ("y", "c"), cross_plus)
    far_own = lax.ppermute(prev_own, "y", plus)
    far_pair = lax.ppermute(next_pair, "y", minus)
    pair = lax.ppermute(sent, "c", swap)

    part = spread(hidden.T, "z", nz).reshape(nz * feat, tok)
    mine = spread(part, "x", nx).reshape(nx * nz * feat, tok)
    theirs = lax.ppermute(mine, "c", swap)

    held = [
        (0, 0, own),
        (0, 1, pair),
        (ny - 1, 0, prev_own),
        (1, 0, next_own),
        (ny - 1, 1, prev_pair),
        (1, 1, next_pair),
        (2, 0, far_own),
        (2, 1, far_pair),
    ]
    blocks = [block for _, _, block in held]
    steps = jnp.array([step for step, _, _ in held], jnp.int32)
    others = jnp.array([other for _, other, _ in held], jnp.int32)
    owner = ((y + steps) % ny) * nc + (c + others) % nc
    place = jnp.concatenate([owner * rows, c[None], y[None]]).astype(jnp.int32)

    both, logits = forward(place, mine, theirs, blocks)
    every = spread(both, ("y", "c"), batch).reshape(ny, nc, nc * queries, half)
    halves = [every[:, i].reshape(batch * queries, half) for i in range(nc)]
    wide = jnp.concatenate(halves, axis=1)
    pooled = lax.dynamic_slice_in_dim(wide, (y * nc + c) * queries, queries, 0)

    slots = pair_query.shape[0]
    n_query, n_passage = batch * queries, passages.shape[0]
    pair_query, pair_passage = pair_query.reshape(1, slots), pair_passage.reshape(1, slots)
    table = dot(passages, wide, 1, 1)
    query_hot = (pair_query == jnp.arange(n_query, dtype=jnp.int32)[:, None]).astype(F32)
    passage_hot = (pair_passage == jnp.arange(n_passage, dtype=jnp.int32)[:, None]).astype(F32)
    spread_table = jnp.dot(table, query_hot, precision=lax.Precision.HIGHEST)
    partial_value = (spread_table * passage_hot).sum(0)
    packed = jnp.pad(partial_value, (0, -slots % 512)).reshape(-1, LANES)
    partials = spread(packed, ("x", "z"), nx * nz)
    positive = jnp.maximum(logits, 0.0)
    slope = jnp.where(logits > 0, 1.0 / (1.0 + positive), 0.0)

    terms = query_terms(
        pair_count,
        partials,
        teacher.reshape(1, slots),
        pair_query,
        pair_passage,
        passages,
        (batch, nc * queries, half + LANES),
    )
    terms = lax.all_to_all(terms, ("y", "c"), 0, 0, tiled=True)

    kept, sent, loss = backward(place, terms, slope, blocks)
    loss_value = (loss[0, 0] + loss[0, LANES - 1]) / (slots * batch)
    other = lax.ppermute(sent, "c", swap)
    hidden_terms = (kept.astype(F32) + other.astype(F32)).astype(BF16)
    hidden_terms = hidden_terms.reshape(nx, nz * feat, tok)
    over_x = lax.all_to_all(hidden_terms, "x", 0, 0, tiled=True)
    over_x = over_x.astype(F32).sum(0).astype(BF16).reshape(nz, feat, tok)
    over_z = lax.all_to_all(over_x, "z", 0, 0, tiled=True)
    grad_hidden = over_z.astype(F32).sum(0).astype(BF16).T
    return (pooled, grad_hidden, loss_value)


def solution(mesh, sizes=(4, 16, 4, 2)):
    mesh = Mesh(mesh.devices.reshape(sizes), ("x", "z", "y", "c"))
    both = P(("y", "c"), ("x", "z"))
    batch = P(("y", "c"))
    return jax.shard_map(
        step,
        mesh=mesh,
        in_specs=(both, both, both, batch, batch, batch, batch),
        out_specs=(both, both, P()),
        check_vma=False,
    )
```

```python
import functools
import math

import jax
import jax.numpy as jnp
from jax import lax
from jax.experimental import pallas as pl
from jax.experimental.pallas import tpu as pltpu
from jax.sharding import Mesh
from jax.sharding import PartitionSpec as P


VOCAB = 65536
QLEN = 16
LANES = 128
F32 = jnp.float32
BF16 = jnp.bfloat16


def ring(n, step):
    return [(i, (i + step) % n) for i in range(n)]


def cross(ny, nc, step):
    return [
        (y * nc + c, ((y + step) % ny) * nc + (c + 1) % nc) for y in range(ny) for c in range(nc)
    ]


def spread(value, axes, n):
    return lax.all_to_all(jnp.broadcast_to(value[None], (n,) + value.shape), axes, 0, 0, tiled=True)


def dot(a, b, ca, cb):
    return lax.dot_general(a, b, (((ca,), (cb,)), ((), ())), preferred_element_type=F32)


ANY = pl.BlockSpec(memory_space=pl.ANY)
SMEM = pl.BlockSpec(memory_space=pltpu.SMEM)
WHOLE = pl.BlockSpec(memory_space=pltpu.VMEM)


def forward_kernel(nb, place, mine, theirs, *refs):
    blocks, (pooled, logits, feats, held, total, sems) = refs[:nb], refs[nb:]
    rows = held.shape[1]
    tok = mine.shape[1]
    copies = []
    for k in range(nb):
        start = pl.multiple_of(place[k], rows)
        near = feats.at[k, :, pl.ds(0, tok)]
        far = feats.at[k, :, pl.ds(tok, tok)]
        copies += [
            pltpu.make_async_copy(blocks[k], held.at[k], sems.at[k]),
            pltpu.make_async_copy(mine.at[pl.ds(start, rows)], near, sems.at[nb + k]),
            pltpu.make_async_copy(theirs.at[pl.ds(start, rows)], far, sems.at[2 * nb + k]),
        ]
    for copy in copies:
        copy.start()
    for k in range(nb):
        for copy in copies[3 * k : 3 * k + 3]:
            copy.wait()
        term = dot(feats[k], held[k], 0, 0)
        if k:
            total[...] += term
        else:
            total[...] = term
    keep = pltpu.make_async_copy(total, logits, sems.at[3 * nb])
    keep.start()
    sums = jnp.log1p(jnp.maximum(total[...], 0.0)).reshape(-1, QLEN, total.shape[1]).sum(1)
    half = sums.shape[0] // 2
    first, second = sums[:half], sums[half:]
    swapped = place[nb] == 1
    pooled[:half, :] = jnp.where(swapped, second, first).astype(BF16)
    pooled[half:, :] = jnp.where(swapped, first, second).astype(BF16)
    keep.wait()


def forward(place, mine, theirs, blocks):
    nb, (rows, cols) = len(blocks), blocks[0].shape
    depth, tok = mine.shape
    queries = 2 * tok // QLEN
    return pl.pallas_call(
        functools.partial(forward_kernel, nb),
        name="forward",
        out_shape=(
            jax.ShapeDtypeStruct((queries, cols), BF16),
            jax.ShapeDtypeStruct((2 * tok, cols), F32),
        ),
        in_specs=[SMEM] + [ANY] * (2 + nb),
        out_specs=(WHOLE, ANY),
        scratch_shapes=[
            pltpu.VMEM((nb, rows, 2 * tok), BF16),
            pltpu.VMEM((nb, rows, cols), BF16),
            pltpu.VMEM((2 * tok, cols), F32),
            pltpu.SemaphoreType.DMA((3 * nb + 1,)),
        ],
        cost_estimate=pl.CostEstimate(
            flops=4 * tok * depth * cols,
            bytes_accessed=2 * depth * (2 * tok + cols) + 8 * tok * cols,
            transcendentals=2 * tok * cols,
        ),
        compiler_params=pltpu.CompilerParams(vmem_limit_bytes=32 << 20),
    )(place, mine, theirs, *blocks)


def terms_kernel(
    pair_count, partials, teacher, pair_query, pair_passage, stored, out, passages, sem
):
    copy = pltpu.make_async_copy(stored, passages, sem)
    copy.start()
    groups, queries, width = out.shape
    half = width - LANES
    cores = passages.shape[1] // half
    slots = pair_query.shape[1]
    inv_root = 1.0 / math.sqrt(VOCAB)
    total = partials[...].astype(F32).sum(0)
    lines = slots // LANES
    scores = jnp.concatenate([total[i : i + 1] for i in range(lines)], axis=1) * inv_root
    is_live = lax.broadcasted_iota(jnp.int32, (1, slots), 1) < pair_count[0]
    residual = jnp.where(is_live, scores - teacher[...], 0.0)
    error = jnp.sum(residual * residual)
    pair_grad = 2.0 * residual * inv_root
    n_query, n_passage = queries * groups // cores, passages.shape[0]
    query_hot = pair_query[...] == lax.broadcasted_iota(jnp.int32, (n_query, slots), 0)
    passage_hot = pair_passage[...] == lax.broadcasted_iota(jnp.int32, (n_passage, slots), 0)
    table = lax.dot_general(
        query_hot.astype(F32),
        jnp.where(passage_hot, pair_grad, 0.0),
        (((1,), (1,)), ((), ())),
        precision=lax.Precision.HIGHEST,
        preferred_element_type=F32,
    )
    high = table.astype(BF16)
    low = (table - high.astype(F32)).astype(BF16)
    parts = jnp.concatenate([high, low], axis=0)
    copy.wait()
    for i in range(cores):
        both = dot(parts, passages[:, i * half : (i + 1) * half], 1, 0)
        terms = both[:n_query] + both[n_query:]
        for k in range(groups // cores):
            out[k * cores + i, :, :half] = terms[k * queries : (k + 1) * queries].astype(BF16)
    errors = jnp.full((groups, queries, LANES), error, F32)
    error_high = errors.astype(BF16)
    error_low = (errors - error_high.astype(F32)).astype(BF16)
    lane = lax.broadcasted_iota(jnp.int32, errors.shape, 2)
    out[:, :, half:] = jnp.where(lane < LANES // 2, error_high, error_low)


def query_terms(pair_count, partials, teacher, pair_query, pair_passage, passages, shape):
    return pl.pallas_call(
        terms_kernel,
        name="query_terms",
        out_shape=jax.ShapeDtypeStruct(shape, BF16),
        in_specs=[SMEM] + [WHOLE] * 4 + [ANY],
        out_specs=WHOLE,
        scratch_shapes=[pltpu.VMEM(passages.shape, BF16), pltpu.SemaphoreType.DMA(())],
        compiler_params=pltpu.CompilerParams(vmem_limit_bytes=16 << 20),
    )(pair_count, partials, teacher, pair_query, pair_passage, passages)


def backward_kernel(nb, place, terms, slope, *refs):
    blocks, (mine, theirs, loss, held, sems) = refs[:nb], refs[nb:]
    rows = blocks[0].shape[0]
    tok, cols = slope.shape
    copies = []
    for k in range(nb):
        start = pl.multiple_of(place[k], rows)
        copies.append(pltpu.make_async_copy(blocks[k], held.at[pl.ds(start, rows)], sems.at[k]))
        copies[k].start()
    total = terms[...].astype(F32).sum(0)
    loss[...] = total[:1, cols:]
    half = total.shape[0] // 2
    swapped = place[nb] == 1
    one, two = total[:half, :cols], total[half:, :cols]
    kept = jnp.concatenate([jnp.where(swapped, two, one), jnp.where(swapped, one, two)], axis=0)
    wide = jnp.broadcast_to(kept[:, None, :], (tok // QLEN, QLEN, cols)).reshape(tok, cols)
    logit_grad = (wide * slope[...]).astype(BF16)
    for copy in copies:
        copy.wait()
    step = 2 * rows
    for start in range(0, nb * rows, step):
        term = dot(held[start : start + step, :], logit_grad, 1, 1).astype(BF16)
        mine[start : start + step, :] = term[:, : tok // 2]
        theirs[start : start + step, :] = term[:, tok // 2 :]


def backward(place, terms, slope, blocks):
    nb, (rows, cols) = len(blocks), blocks[0].shape
    tok = slope.shape[0]
    depth = nb * rows
    return pl.pallas_call(
        functools.partial(backward_kernel, nb),
        name="backward",
        out_shape=(
            jax.ShapeDtypeStruct((depth, tok // 2), BF16),
            jax.ShapeDtypeStruct((depth, tok // 2), BF16),
            jax.ShapeDtypeStruct((1, LANES), F32),
        ),
        in_specs=[SMEM, WHOLE, WHOLE] + [ANY] * nb,
        out_specs=(WHOLE,) * 3,
        scratch_shapes=[
            pltpu.VMEM((depth, cols), BF16),
            pltpu.SemaphoreType.DMA((nb,)),
        ],
        cost_estimate=pl.CostEstimate(
            flops=2 * tok * depth * cols,
            bytes_accessed=2 * depth * (tok + cols) + 4 * tok * cols,
            transcendentals=0,
        ),
        compiler_params=pltpu.CompilerParams(vmem_limit_bytes=32 << 20),
    )(place, terms, slope, *blocks)


def step(hidden, head, passages, pair_query, pair_passage, pair_count, teacher):
    nx, nz = lax.axis_size("x"), lax.axis_size("z")
    ny, nc = lax.axis_size("y"), lax.axis_size("c")
    y, c = lax.axis_index("y"), lax.axis_index("c")
    tok, feat = hidden.shape
    rows, cols = head.shape
    half = cols // nc
    batch = ny * nc
    queries = tok // QLEN
    swap = ring(nc, 1)
    plus, minus = ring(ny, 1), ring(ny, ny - 1)

    own = lax.dynamic_slice_in_dim(head, c * half, half, 1)
    sent = lax.dynamic_slice_in_dim(head, (1 - c) * half, half, 1)
    cross_plus, cross_minus = cross(ny, nc, 1), cross(ny, nc, ny - 1)
    next_pair = lax.ppermute(sent, ("y", "c"), cross_minus)
    prev_own = lax.ppermute(own, "y", plus)
    next_own = lax.ppermute(own, "y", minus)
    prev_pair = lax.ppermute(sent, ("y", "c"), cross_plus)
    far_own = lax.ppermute(prev_own, "y", plus)
    far_pair = lax.ppermute(next_pair, "y", minus)
    pair = lax.ppermute(sent, "c", swap)

    part = spread(hidden.T, "z", nz).reshape(nz * feat, tok)
    mine = spread(part, "x", nx).reshape(nx * nz * feat, tok)
    theirs = lax.ppermute(mine, "c", swap)

    held = [
        (0, 0, own),
        (0, 1, pair),
        (ny - 1, 0, prev_own),
        (1, 0, next_own),
        (ny - 1, 1, prev_pair),
        (1, 1, next_pair),
        (2, 0, far_own),
        (2, 1, far_pair),
    ]
    blocks = [block for _, _, block in held]
    steps = jnp.array([step for step, _, _ in held], jnp.int32)
    others = jnp.array([other for _, other, _ in held], jnp.int32)
    owner = ((y + steps) % ny) * nc + (c + others) % nc
    place = jnp.concatenate([owner * rows, c[None], y[None]]).astype(jnp.int32)

    both, logits = forward(place, mine, theirs, blocks)
    every = spread(both, ("y", "c"), batch).reshape(ny, nc, nc * queries, half)
    halves = [every[:, i].reshape(batch * queries, half) for i in range(nc)]
    wide = jnp.concatenate(halves, axis=1)
    pooled = lax.dynamic_slice_in_dim(wide, (y * nc + c) * queries, queries, 0)

    slots = pair_query.shape[0]
    n_query, n_passage = batch * queries, passages.shape[0]
    pair_query, pair_passage = pair_query.reshape(1, slots), pair_passage.reshape(1, slots)
    table = dot(passages, wide, 1, 1)
    query_hot = (pair_query == jnp.arange(n_query, dtype=jnp.int32)[:, None]).astype(F32)
    passage_hot = (pair_passage == jnp.arange(n_passage, dtype=jnp.int32)[:, None]).astype(F32)
    spread_table = jnp.dot(table, query_hot, precision=lax.Precision.HIGHEST)
    partial_value = (spread_table * passage_hot).sum(0)
    packed = jnp.pad(partial_value, (0, -slots % 512)).reshape(-1, LANES).astype(BF16)
    partials = spread(packed, ("x", "z"), nx * nz)
    positive = jnp.maximum(logits, 0.0)
    slope = jnp.where(logits > 0, 1.0 / (1.0 + positive), 0.0)

    terms = query_terms(
        pair_count,
        partials,
        teacher.reshape(1, slots),
        pair_query,
        pair_passage,
        passages,
        (batch, nc * queries, half + LANES),
    )
    terms = lax.all_to_all(terms, ("y", "c"), 0, 0, tiled=True)

    kept, sent, loss = backward(place, terms, slope, blocks)
    loss_value = (loss[0, 0] + loss[0, LANES - 1]) / (slots * batch)
    other = lax.ppermute(sent, "c", swap)
    hidden_terms = (kept.astype(F32) + other.astype(F32)).astype(BF16)
    hidden_terms = hidden_terms.reshape(nx, nz * feat, tok)
    over_x = lax.all_to_all(hidden_terms, "x", 0, 0, tiled=True)
    over_x = over_x.astype(F32).sum(0).astype(BF16).reshape(nz, feat, tok)
    over_z = lax.all_to_all(over_x, "z", 0, 0, tiled=True)
    grad_hidden = over_z.astype(F32).sum(0).astype(BF16).T
    return (pooled, grad_hidden, loss_value)


def solution(mesh, sizes=(4, 16, 4, 2)):
    mesh = Mesh(mesh.devices.reshape(sizes), ("x", "z", "y", "c"))
    both = P(("y", "c"), ("x", "z"))
    batch = P(("y", "c"))
    return jax.shard_map(
        step,
        mesh=mesh,
        in_specs=(both, both, both, batch, batch, batch, batch),
        out_specs=(both, both, P()),
        check_vma=False,
    )
```
